256 devices in a mesh: node: 32 (over x, z_hi, core), col: 8 (over z_lo, y).
Axes of the slice: x: 4, y: 4, z: 8 (z_hi: 4, z_lo: 2; z = z_hi * 2 + z_lo), core: 2. Of those that a mesh axis runs over, the one named last changes fastest.
Arguments:
- coefficients: float32 [8, 128, 256, 1024], P('col', 'node'), may hold values from -6 to 6
- self_weights: bfloat16 [8, 6, 128, 256, 256], P('col', None, 'node'), may hold values from -0.25 to 0.25
- cross_weights: bfloat16 [8, 6, 128, 256, 256], P('col', None, 'node'), may hold values from -0.25 to 0.25
- true_ranks: int32 [8, 128], P('col', 'node'), may hold values from 128 to 256
Outputs:
- field: float32 [128, 256, 1024], P('node', None, 'col')
The draws below stay inside these ranges and needn't reach their ends.
Inputs may be any that keep to these rules, and one draw needn't show every extreme that they name: `true_ranks`: each node's true rank within its padded rank 256.
All inputs are finite; a program needn't handle non-finite values.
Results may differ from the reference program's by a relative error of at most 0.0003.
Values sent between devices are 32-bit elements; how exact they have to be, the bound alone decides.
No kernel may reach another device: no remote copies, remote signals or barrier semaphores. Data moves between devices by JAX's collectives and lax.ppermute only.
A program may use at most 64 MiB of HBM per device.

```python
import jax
import jax.numpy as jnp
from jax import lax

RANK = 256
ILLUM = 1024
LEVELS = 6
NODES = 128
COLS = 8


def place_ends(result, own_key, smallest, top_value):
    longest = result.shape.index(max(result.shape))
    spots = []
    for shift in (0, 1):
        where = [jax.random.randint(jax.random.fold_in(own_key, axis), (), 0, length) for axis, length in enumerate(result.shape)]
        where[longest] = (where[longest] + shift) % result.shape[longest]
        spots.append(tuple(where))
    return result.at[spots[0]].set(smallest).at[spots[1]].set(top_value)


def block_scale(key, extent, shards, smallest, high):
    def one(position, parts):
        steps = jax.random.uniform(jax.random.fold_in(jax.random.fold_in(key, 6), position), (parts,), jnp.float32, smallest / len(shards), high / len(shards))
        return jnp.repeat(jnp.exp(steps), extent[position] // parts).reshape((-1,) + (1,) * (len(extent) - position - 1))

    loudness = one(*shards[0])
    for cut in shards[1:]:
        loudness = loudness * one(*cut)
    return loudness


def gaussian(own_key, dims, deviation, reach, split=(), held_as=jnp.bfloat16):
    drawn = jax.random.normal(own_key, dims, jnp.float32) * deviation
    if len(split) > 0:
        drawn = block_scale(own_key, dims, split, -0.22, 0.18) * drawn
    return jnp.clip(drawn, min=-reach, max=reach).astype(held_as)


def setup_inputs(seed: int = 0) -> dict:
    key_list = jax.random.split(jax.random.key(seed), 5)
    return {
        "coefficients": gaussian(key_list[0], (COLS, NODES, RANK, ILLUM), 1.0, 6.0, ((0, 8), (1, 32)), jnp.float32),
        "self_weights": gaussian(key_list[1], (COLS, LEVELS, NODES, RANK, RANK), (2 * RANK) ** -0.5, 0.25, ((0, 8), (2, 32))),
        "cross_weights": gaussian(key_list[2], (COLS, LEVELS, NODES, RANK, RANK), (2 * RANK) ** -0.5, 0.25, ((0, 8), (2, 32))),
        "true_ranks": place_ends(jax.random.randint(key_list[3], (COLS, NODES), RANK // 2, RANK + 1), jax.random.fold_in(key_list[3], 1), RANK // 2, RANK).astype(jnp.int32),
    }


def apply_mats(weights, coeffs):
    return jnp.einsum("nrk,nki->nri", weights.astype(jnp.float32), coeffs, precision=lax.Precision.HIGHEST)


def partner_view(values, section):
    node_count = values.shape[0]
    shaped = values.reshape((node_count >> (section + 1), 2, 1 << section) + values.shape[1:])
    return shaped[:, ::-1].reshape(values.shape)


def reference(coefficients, self_weights, cross_weights, true_ranks):
    def column(running, items):
        coeffs, self_mats, cross_mats, rank_vec = items
        row_index = lax.broadcasted_iota(jnp.int32, (coeffs.shape[0], coeffs.shape[1], 1), 1)
        row_keep = (row_index < rank_vec.astype(jnp.int32)[:, None, None]).astype(jnp.float32)
        for section in range(LEVELS):
            self_term = apply_mats(self_mats[section], coeffs)
            sent_term = apply_mats(cross_mats[section], coeffs)
            coeffs = row_keep * (self_term + partner_view(sent_term, section))
        return running + coeffs, None

    start = jnp.zeros(coefficients.shape[1:], jnp.float32)
    running, _ = lax.scan(column, start, (coefficients, self_weights, cross_weights, true_ranks))
    return running
```

```python
import jax
import jax.numpy as jnp
from jax import lax
from jax.experimental import pallas as pl
from jax.experimental.pallas import tpu as pltpu
from jax.sharding import PartitionSpec as P

F32 = jnp.float32
BF16 = jnp.bfloat16
VMEM_LIMIT = 48 * 1024 * 1024


def params():
    return pltpu.CompilerParams(vmem_limit_bytes=VMEM_LIMIT)


SMALL = pl.CostEstimate(flops=1000, bytes_accessed=1000, transcendentals=0)


def split(state):
    hi = state.astype(BF16)
    return hi, (state - hi.astype(F32)).astype(BF16)


def times(weight, parts):
    hi, lo = parts
    return jnp.dot(weight, hi, preferred_element_type=F32) + jnp.dot(
        weight, lo, preferred_element_type=F32
    )


def masked(rank, value):
    return jnp.where(lax.broadcasted_iota(jnp.int32, value.shape, 0) < rank, value, 0.0)


def local_kernel(ranks, state, self_w, cross_w, keep_out, send_out):
    count = state.shape[1]
    nodes = [state[0, n] for n in range(count)]
    for level in range(2):
        parts = [split(v) for v in nodes]
        kept = [times(self_w[0, level, n], parts[n]) for n in range(count)]
        sent = [times(cross_w[0, level, n], parts[n]) for n in range(count)]
        nodes = [masked(ranks[n], kept[n] + sent[n ^ (1 << level)]) for n in range(count)]
    for n in range(count):
        parts = split(nodes[n])
        keep_out[n] = times(self_w[0, 2, n], parts)
        send_out[n] = times(cross_w[0, 2, n], parts)


def local_levels(part, parts, coefficients, self_weights, cross_weights, ranks):
    _, count, rank, illum = coefficients.shape
    width = illum // parts
    block = 256
    steps = width // block
    mats = pl.BlockSpec((1, 3, count, rank, rank), lambda i, r: (0, 0, 0, 0, 0))
    out = pl.BlockSpec((count, rank, block), lambda i, r: (0, 0, i))
    return pl.pallas_call(
        local_kernel,
        grid_spec=pltpu.PrefetchScalarGridSpec(
            num_scalar_prefetch=1,
            grid=(steps,),
            in_specs=[
                pl.BlockSpec((1, count, rank, block), lambda i, r: (0, 0, 0, part * steps + i)),
                mats,
                mats,
            ],
            out_specs=[out, out],
        ),
        out_shape=[jax.ShapeDtypeStruct((count, rank, width), F32)] * 2,
        compiler_params=params(),
        cost_estimate=SMALL,
        name=f"local_part{part}",
    )(ranks, coefficients, self_weights, cross_weights)


def level3_kernel(node, info, kept, recv, self_w, cross_w, keep_out, send_out):
    parts = split(masked(info[node], kept[0] + recv[0]))
    mine = times(self_w[0, 0, 0], parts)
    other = times(cross_w[0, 0, 0], parts)
    flag = info[4]

    @pl.when(flag == 0)
    def _():
        keep_out[...] = mine
        send_out[...] = other

    @pl.when(flag != 0)
    def _():
        keep_out[...] = other
        send_out[...] = mine


def level3(node, part, info, kept, recv, self_weights, cross_weights):
    _, rank, width = kept.shape
    block = 256
    tile = pl.BlockSpec((1, rank, block), lambda i, r: (node, 0, i))
    mat = pl.BlockSpec((1, 1, 1, rank, rank), lambda i, r: (0, 3, node, 0, 0))
    out = pl.BlockSpec((rank, block), lambda i, r: (0, i))
    return pl.pallas_call(
        lambda *refs: level3_kernel(node, *refs),
        grid_spec=pltpu.PrefetchScalarGridSpec(
            num_scalar_prefetch=1,
            grid=(width // block,),
            in_specs=[tile, tile, mat, mat],
            out_specs=[out, out],
        ),
        out_shape=[jax.ShapeDtypeStruct((rank, width), F32)] * 2,
        compiler_params=params(),
        cost_estimate=SMALL,
        name=f"level3_{node}{part}",
    )(info, kept, recv, self_weights, cross_weights)


def moved_kernel(node, info, kept, recv, self_w, cross_w, moved, keep_out, send_out, mats):
    @pl.when(pl.program_id(0) == 0)
    def _():
        @pl.when(info[4] == 0)
        def _():
            mats[0] = self_w[0, 0, 0]
            mats[1] = cross_w[0, 0, 0]

        @pl.when(info[4] != 0)
        def _():
            mats[0] = moved[0].astype(BF16)
            mats[1] = moved[1].astype(BF16)

    parts = split(masked(info[node], kept[...] + recv[...]))
    keep_out[...] = times(mats[0], parts)
    send_out[...] = times(mats[1], parts)


def moved_level(level, node, part, info, kept, recv, self_weights, cross_weights, moved):
    rank, width = kept.shape
    block = 256
    tile = pl.BlockSpec((rank, block), lambda i, r: (0, i))
    mat = pl.BlockSpec((1, 1, 1, rank, rank), lambda i, r: (0, level, node, 0, 0))
    return pl.pallas_call(
        lambda *refs: moved_kernel(node, *refs),
        grid_spec=pltpu.PrefetchScalarGridSpec(
            num_scalar_prefetch=1,
            grid=(width // block,),
            in_specs=[tile, tile, mat, mat, pl.BlockSpec((2, rank, rank), lambda i, r: (0, 0, 0))],
            out_specs=[tile, tile],
            scratch_shapes=[pltpu.VMEM((2, rank, rank), BF16)],
        ),
        out_shape=[jax.ShapeDtypeStruct((rank, width), F32)] * 2,
        compiler_params=params(),
        cost_estimate=SMALL,
        name=f"level{level}_{node}{part}",
    )(info, kept, recv, self_weights, cross_weights, moved)


def halve_kernel(node, spot, info, kept_a, recv_a, kept_b, recv_b, keep_out, send_out):
    for kept, recv, out in ((kept_a, recv_a, keep_out), (kept_b, recv_b, send_out)):
        total = kept[...] + recv[...]
        out[...] = total if node is None else masked(info[node], total)


def halve(node, spot, info, kept, recv):
    rank, width = kept.shape
    block = width // 2
    mine = pl.BlockSpec((rank, block), lambda i, s, r: (0, s[0]))
    theirs = pl.BlockSpec((rank, block), lambda i, s, r: (0, s[1]))
    out = pl.BlockSpec((rank, block), lambda i, s, r: (0, 0))
    return pl.pallas_call(
        lambda *refs: halve_kernel(node, *refs),
        grid_spec=pltpu.PrefetchScalarGridSpec(
            num_scalar_prefetch=2,
            grid=(1,),
            in_specs=[mine, mine, theirs, theirs],
            out_specs=[out, out],
        ),
        out_shape=[jax.ShapeDtypeStruct((rank, block), F32)] * 2,
        compiler_params=params(),
        cost_estimate=SMALL,
        name="halve",
    )(spot, info, kept, recv, kept, recv)


def swap(value, axis, mask, chosen=lambda index: True):
    pairs = [(i, i ^ mask) for i in range(lax.axis_size(axis)) if chosen(i)]
    return lax.ppermute(value, axis, pairs)


def tie(value, *before):
    return lax.optimization_barrier((value, *before))[0]


CORE, Z1, Z2, X0 = 1, 2, 4, 8
PARTS = 2


def moves(index):
    return (index & 1) == ((index >> 2) & 1)


def shards(coefficients, self_weights, cross_weights, true_ranks):
    ranks = true_ranks[0]
    count = ranks.shape[0]
    nodes, cols = lax.axis_size("node"), lax.axis_size("col")
    flag = moves(lax.axis_index("node")).astype(jnp.int32)
    col = lax.axis_index("col")
    y0, y1, z0 = col & 1, (col >> 1) & 1, (col >> 2) & 1
    spot_y1 = jnp.stack([y1, 1 - y1]).astype(jnp.int32)
    spot_y0 = jnp.stack([y0, 1 - y0]).astype(jnp.int32)

    held = jnp.where(flag == 1, swap(ranks, "node", Z1, moves), ranks)
    own_info = jnp.concatenate([ranks, flag[None]])
    held_info = jnp.concatenate([held, flag[None]])

    def wide(level, node):
        pair = jnp.stack([self_weights[0, level, node], cross_weights[0, level, node]])
        return pair.astype(F32)

    def fetch(level, node, *before):
        return swap(tie(wide(level, node), *before), "node", Z1, moves)

    early = [(4, 0), (5, 0), (4, 1)]
    start_ranks, *mats = lax.optimization_barrier((ranks, *[wide(*key) for key in early]))
    moved = {key: swap(mat, "node", Z1, moves) for key, mat in zip(early, mats)}
    later = [(5, 1), (4, 2), (5, 2), (4, 3), (5, 3)]

    first = []
    for part in range(PARTS):
        k, s = local_levels(part, PARTS, coefficients, self_weights, cross_weights, start_ranks)
        first.append((k, swap(s, "node", CORE)))

    pieces = [(node, part) for node in range(count) for part in range(PARTS)]
    gates = [moved[4, 0], moved[5, 0]]
    done = {}

    def past(*keys):
        return [done[key] for key in keys if key in done]

    sums, results = {}, []
    for turn, (node, part) in enumerate(pieces):
        k, s = level3(node, part, own_info, *first[part], self_weights, cross_weights)
        gates += past((5, turn - 4), (6, turn - 5), (7, turn - 6))
        s = tie(s, *gates)
        if turn < len(later):
            moved[later[turn]] = fetch(*later[turn], *gates)
        r = swap(s, "node", Z1)
        gates = [r, moved[4, 1]] if turn == 0 else [r]
        if turn < len(later):
            gates.append(moved[later[turn]])
        k, s = moved_level(4, node, part, held_info, k, r, self_weights, cross_weights, moved[4, node])
        s = tie(s, *past((4, turn - 2)))
        r = done[4, turn] = swap(s, "node", Z1 | Z2)
        k, s = moved_level(5, node, part, held_info, k, r, self_weights, cross_weights, moved[5, node])
        r = done[5, turn] = swap(s, "node", X0)
        k, s = halve(node, spot_y1, held_info, k, r)
        r = done[6, turn] = swap(s, "col", 2)
        k, s = halve(None, spot_y0, held_info, k, r)
        r = done[7, turn] = swap(s, "col", 1)
        sums[part] = k + r
        if part == PARTS - 1:
            mine = jnp.where(z0 == 1, sums[1], sums[0])
            theirs = jnp.where(z0 == 1, sums[0], sums[1])
            home, across = [], []
            for d in range(nodes):
                for c in range(cols):
                    to = d ^ Z1 if moves(d) else d
                    across.append((d * cols + c, to * cols + (c ^ 4)))
                    if moves(d):
                        home.append((d * cols + c, to * cols + c))
            away = lax.ppermute(mine, ("node", "col"), home)
            other = lax.ppermute(theirs, ("node", "col"), across)
            results.append(jnp.where(flag == 1, away, mine) + other)
    return jnp.stack(results)


def solution(mesh):
    placed = (
        P("col", "node", None, None),
        P("col", None, "node", None, None),
        P("col", None, "node", None, None),
        P("col", "node"),
    )
    return jax.shard_map(
        shards, mesh=mesh, in_specs=placed, out_specs=P("node", None, "col"), check_vma=False
    )
```

```python
import jax
import jax.numpy as jnp
from jax import lax
from jax.experimental import pallas as pl
from jax.experimental.pallas import tpu as pltpu
from jax.sharding import PartitionSpec as P

F32 = jnp.float32
BF16 = jnp.bfloat16
VMEM_LIMIT = 48 * 1024 * 1024


def params():
    return pltpu.CompilerParams(vmem_limit_bytes=VMEM_LIMIT)


COST = pl.CostEstimate(flops=10**11, bytes_accessed=10**9, transcendentals=0)


def split(state):
    hi = state.astype(BF16)
    return jnp.concatenate([hi, (state - hi.astype(F32)).astype(BF16)], axis=0)


def times(weight, pieces):
    doubled = jnp.concatenate([weight, weight], axis=1)
    return jnp.dot(doubled, pieces, preferred_element_type=F32)


def masked(rank, value):
    return jnp.where(lax.broadcasted_iota(jnp.int32, value.shape, 0) < rank, value, 0.0)


def hbm(*shape):
    return pltpu.HBM(shape, F32)


def placed(*arrays):
    return [pltpu.with_memory_space_constraint(array, pltpu.HBM) for array in arrays]


def local_kernel(ranks, state, self_w, cross_w, keep_out, send_out):
    count = state.shape[1]
    nodes = [state[0, n] for n in range(count)]
    for level in range(2):
        parts = [split(v) for v in nodes]
        kept = [times(self_w[0, level, n], parts[n]) for n in range(count)]
        sent = [times(cross_w[0, level, n], parts[n]) for n in range(count)]
        nodes = [masked(ranks[n], kept[n] + sent[n ^ (1 << level)]) for n in range(count)]
    for n in range(count):
        parts = split(nodes[n])
        keep_out[n] = times(self_w[0, 2, n], parts)
        send_out[n] = times(cross_w[0, 2, n], parts)


def local_levels(part, parts, coefficients, self_weights, cross_weights, ranks):
    _, count, rank, illum = coefficients.shape
    width = illum // parts
    block = 256
    steps = width // block
    mats = pl.BlockSpec((1, 3, count, rank, rank), lambda i, r: (0, 0, 0, 0, 0))
    out = pl.BlockSpec((count, rank, block), lambda i, r: (0, 0, i))
    return pl.pallas_call(
        local_kernel,
        grid_spec=pltpu.PrefetchScalarGridSpec(
            num_scalar_prefetch=1,
            grid=(steps,),
            in_specs=[
                pl.BlockSpec((1, count, rank, block), lambda i, r: (0, 0, 0, part * steps + i)),
                mats,
                mats,
            ],
            out_specs=[out, out],
        ),
        out_shape=[hbm(count, rank, width)] * 2,
        compiler_params=params(),
        cost_estimate=COST,
        name=f"local_part{part}",
    )(ranks, *placed(coefficients, self_weights, cross_weights))


def widen_kernel(self_w, cross_w, *outs):
    each = 2 // len(outs)
    for n in range(2):
        outs[n // each][n % each, 0] = self_w[0, n, 0].astype(F32)
        outs[n // each][n % each, 1] = cross_w[0, n, 0].astype(F32)


def widen(node, arrays, self_weights, cross_weights):
    rank = self_weights.shape[-1]
    shape = (2 // arrays, 2, rank, rank)
    mats = pl.BlockSpec((1, 2, 1, rank, rank), lambda i: (0, 2, node, 0, 0))
    return pl.pallas_call(
        widen_kernel,
        grid=(1,),
        in_specs=[mats, mats],
        out_specs=[pl.BlockSpec(shape, lambda i: (0, 0, 0, 0))] * arrays,
        out_shape=[hbm(*shape)] * arrays,
        compiler_params=params(),
        cost_estimate=COST,
        name=f"widen_{node}",
    )(*placed(self_weights, cross_weights))


def level3_kernel(node, count, info, *refs):
    self_w, cross_w, keep_out, send_out = refs[2 * count :]
    taken = info[4] != 0
    keep_w = jnp.where(taken, cross_w[0, 0, 0], self_w[0, 0, 0])
    send_w = jnp.where(taken, self_w[0, 0, 0], cross_w[0, 0, 0])
    step = pl.program_id(0)
    steps = pl.num_programs(0) // count
    for c in range(count):

        @pl.when(step // steps == c)
        def _():
            parts = split(masked(info[node], refs[2 * c][0] + refs[2 * c + 1][0]))
            keep_out[...] = times(keep_w, parts)
            send_out[...] = times(send_w, parts)


def level3(node, info, pairs, self_weights, cross_weights):
    _, rank, width = pairs[0][0].shape
    count = len(pairs)
    block = 256
    steps = width // block

    def tiles(c):
        def at(i):
            return jnp.clip(i - c * steps, 0, steps - 1)

        return [pl.BlockSpec((1, rank, block), lambda i, r: (node, 0, at(i)))] * 2

    mat = pl.BlockSpec((1, 1, 1, rank, rank), lambda i, r: (0, 3, node, 0, 0))
    out = pl.BlockSpec((rank, block), lambda i, r: (0, i))
    return pl.pallas_call(
        lambda *refs: level3_kernel(node, count, *refs),
        grid_spec=pltpu.PrefetchScalarGridSpec(
            num_scalar_prefetch=1,
            grid=(count * steps,),
            in_specs=[tile for c in range(count) for tile in tiles(c)] + [mat, mat],
            out_specs=[out, out],
        ),
        out_shape=[hbm(rank, count * width)] * 2,
        compiler_params=params(),
        cost_estimate=COST,
        name=f"level3_{node}",
    )(info, *[v for pair in pairs for v in pair], *placed(self_weights, cross_weights))


def moved_kernel(node, count, info, *refs):
    self_w, cross_w, moved, keep_out, send_out, mats = refs[2 * count :]
    step = pl.program_id(0)

    @pl.when(step == 0)
    def _():
        @pl.when(info[4] == 0)
        def _():
            mats[0] = self_w[0, 0, 0]
            mats[1] = cross_w[0, 0, 0]

        @pl.when(info[4] != 0)
        def _():
            mats[0] = moved[0, 0].astype(BF16)
            mats[1] = moved[0, 1].astype(BF16)

    steps = pl.num_programs(0) // count
    for c in range(count):

        @pl.when(step // steps == c)
        def _():
            parts = split(masked(info[node], refs[2 * c][...] + refs[2 * c + 1][...]))
            keep_out[...] = times(mats[0], parts)
            send_out[...] = times(mats[1], parts)


def moved_level(level, node, info, pairs, self_weights, cross_weights, moved):
    rank, width = pairs[0][0].shape
    count = len(pairs)
    block = 256
    steps = width // block
    spot = level - 4 if moved.shape[0] == 2 else 0

    def tile(c):
        return pl.BlockSpec(
            (rank, block), lambda i, r: (0, jnp.clip(i - c * steps, 0, steps - 1))
        )

    mat = pl.BlockSpec((1, 1, 1, rank, rank), lambda i, r: (0, level, node, 0, 0))
    out = pl.BlockSpec((rank, block), lambda i, r: (0, i))
    return pl.pallas_call(
        lambda *refs: moved_kernel(node, count, *refs),
        grid_spec=pltpu.PrefetchScalarGridSpec(
            num_scalar_prefetch=1,
            grid=(count * steps,),
            in_specs=[tile(c) for c in range(count) for _ in range(2)]
            + [mat, mat, pl.BlockSpec((1, 2, rank, rank), lambda i, r: (spot, 0, 0, 0))],
            out_specs=[out, out],
            scratch_shapes=[pltpu.VMEM((2, rank, rank), BF16)],
        ),
        out_shape=[hbm(rank, count * width)] * 2,
        compiler_params=params(),
        cost_estimate=COST,
        name=f"level{level}_{node}",
    )(info, *[v for pair in pairs for v in pair], *placed(self_weights, cross_weights), moved)


def total_kernel(node, count, info, *refs):
    out = refs[-1]
    step = pl.program_id(0)
    steps = pl.num_programs(0) // count
    block = out.shape[2]
    for c in range(count):

        @pl.when(step // steps == c)
        def _():
            value = masked(info[node], refs[2 * c][...] + refs[2 * c + 1][...])
            for j in range(out.shape[0]):
                out[j] = value[:, j * block : (j + 1) * block]


def total(node, info, pairs, cols):
    rank, width = pairs[0][0].shape
    count = len(pairs)
    block = count * width // cols
    each = 4
    steps = cols // (count * each)

    def tile(c):
        return pl.BlockSpec(
            (rank, each * block), lambda i, r: (0, jnp.clip(i - c * steps, 0, steps - 1))
        )

    return pl.pallas_call(
        lambda *refs: total_kernel(node, count, *refs),
        grid_spec=pltpu.PrefetchScalarGridSpec(
            num_scalar_prefetch=1,
            grid=(count * steps,),
            in_specs=[tile(c) for c in range(count) for _ in range(2)],
            out_specs=pl.BlockSpec((each, rank, block), lambda i, r: (i, 0, 0)),
        ),
        out_shape=hbm(cols, rank, block),
        compiler_params=params(),
        cost_estimate=COST,
        name=f"total_{node}",
    )(info, *[v for pair in pairs for v in pair])


def swap(value, axis, mask, chosen=lambda index: True):
    pairs = [(i, i ^ mask) for i in range(lax.axis_size(axis)) if chosen(i)]
    return lax.ppermute(value, axis, pairs)


def tie(value, *before):
    return lax.optimization_barrier((value, *before))[0]


CORE, Z1, Z2, X0 = 1, 2, 4, 8
PARTS = 2


def moves(index):
    return (index & 1) == ((index >> 2) & 1)


def shards(coefficients, self_weights, cross_weights, true_ranks):
    ranks = true_ranks[0]
    count = ranks.shape[0]
    cols = lax.axis_size("col")
    flag = moves(lax.axis_index("node")).astype(jnp.int32)
    weights = (self_weights, cross_weights)

    wide = [widen(0, 1, *weights)[0]]
    moved = {0: swap(wide[0], "node", Z1, moves)}
    fetches, arrivals = {0: 1, 2: 2, 5: 3}, {3: 1, 5: 2, 7: 3}
    sends = {1: 2, 2: 3, 3: 4, 4: 5, 6: 6, 7: 7}
    pieces = [(node, part) for node in range(count) for part in range(PARTS)]
    final = len(pieces)

    own_info = jnp.concatenate([ranks, flag[None]])
    kept3, sent3 = {}, {}
    first = []
    for part in range(PARTS):
        start = tie(ranks, sent3[0] if part else wide[0])
        k, sent = local_levels(part, PARTS, coefficients, *weights, start)
        first.append((k, swap(sent, "node", CORE)))
        kept3[part], sent3[part] = level3(0, own_info, [first[part]], *weights)
    later_ranks, later_weights = tie(ranks, sent3[0]), tie(self_weights, sent3[0])
    wide += [widen(node, 1, later_weights, cross_weights)[0] for node in range(1, count)]
    other_ranks = swap(later_ranks, "node", Z1, moves)
    held = jnp.where(flag == 1, other_ranks, ranks)
    held_info = jnp.concatenate([held, flag[None]])

    def third(turn):
        node, part = pieces[turn]
        return level3(node, own_info, [first[part]], *weights)

    def fourth(turn):
        node = pieces[turn][0]
        k, s = moved_level(4, node, held_info, [(kept3[turn], r3[turn])], *weights, moved[node])
        kept4[turn], r4[turn] = k, swap(s, "node", Z1 | Z2)

    def fifth(node, turns):
        state = [(kept4[t], r4[t]) for t in turns]
        k, s = moved_level(5, node, held_info, state, *weights, moved[node])
        return k, swap(s, "node", X0)

    def homeward(group):
        mine = jnp.stack(group)
        return jnp.where(flag == 1, swap(mine, "node", Z1, moves), mine)

    for turn in range(PARTS, final):
        kept3[turn], sent3[turn] = third(turn)
    r3 = {turn: swap(sent3[turn], "node", Z1) for turn in (0, 1)}
    moved[1] = swap(tie(wide[1], sent3[1]), "node", Z1, moves)
    kept4, r4, fives, sums = {}, {}, {}, []

    def column_sum(node, terms):
        blocks = total(node, held_info, terms, cols)
        sums.append(jnp.sum(lax.all_to_all(blocks, "col", 0, 0, tiled=True), axis=0))

    for turn in range(1, final):
        values = {"r3": r3[turn - 1]}
        if turn in sends:
            values["sent3"] = sent3[sends[turn]]
        if turn in fetches:
            values["wide"] = wide[fetches[turn]]
        if turn in arrivals:
            values["moved"] = moved[arrivals[turn]]
        if turn >= 2:
            values["r4"] = r4[turn - 2]
        if turn == 6:
            values["sum"] = sums[0]
        summed = {4: 0, 6: 1}.get(turn)
        if summed is not None:
            values["five"] = fives[summed][1]
        values = dict(zip(values, lax.optimization_barrier(tuple(values.values()))))
        r3[turn - 1] = values["r3"]
        if turn in sends:
            r3[sends[turn]] = swap(values["sent3"], "node", Z1)
        if turn in arrivals:
            moved[arrivals[turn]] = values["moved"]
        if turn in fetches:
            moved[fetches[turn]] = swap(values["wide"], "node", Z1, moves)
        if turn >= 2:
            r4[turn - 2] = values["r4"]
        if turn == 6:
            sums[0] = values["sum"]
        fourth(turn - 1)
        if turn in (3, 5, 7):
            node = (turn - 3) // 2
            fives[node] = fifth(node, [turn - 3, turn - 2])
        if summed is not None:
            column_sum(summed, [(fives[summed][0], values["five"])])

    r3[final - 1], sums[1] = lax.optimization_barrier((r3[final - 1], sums[1]))
    fourth(final - 1)
    ends = [fifth(count - 1, [final - 2]), fifth(count - 1, [final - 1])]
    for node, terms in ((count - 2, [fives[count - 2]]), (count - 1, ends)):
        column_sum(node, terms)
    return jnp.concatenate([homeward(sums[: count - 1]), homeward(sums[count - 1 :])])


def solution(mesh):
    placed = (
        P("col", "node", None, None),
        P("col", None, "node", None, None),
        P("col", None, "node", None, None),
        P("col", "node"),
    )
    return jax.shard_map(
        shards, mesh=mesh, in_specs=placed, out_specs=P("node", None, "col"), check_vma=False
    )
```

```python
import jax
import jax.numpy as jnp
from jax import lax
from jax.experimental import pallas as pl
from jax.experimental.pallas import tpu as pltpu
from jax.sharding import PartitionSpec as P

F32 = jnp.float32
BF16 = jnp.bfloat16
VMEM_LIMIT = 48 * 1024 * 1024


def params():
    return pltpu.CompilerParams(vmem_limit_bytes=VMEM_LIMIT)


COST = pl.CostEstimate(flops=10**11, bytes_accessed=10**9, transcendentals=0)


def split(state):
    hi = state.astype(BF16)
    return jnp.concatenate([hi, (state - hi.astype(F32)).astype(BF16)], axis=0)


def times(weight, pieces):
    doubled = jnp.concatenate([weight, weight], axis=1)
    return jnp.dot(doubled, pieces, preferred_element_type=F32)


def masked(rank, value):
    return jnp.where(lax.broadcasted_iota(jnp.int32, value.shape, 0) < rank, value, 0.0)


def hbm(*shape):
    return pltpu.HBM(shape, F32)


def placed(*arrays):
    return [pltpu.with_memory_space_constraint(array, pltpu.HBM) for array in arrays]


def local_kernel(ranks, state, self_w, cross_w, keep_out, *send_outs):
    count = state.shape[1]
    nodes = [state[0, n] for n in range(count)]
    for level in range(2):
        parts = [split(v) for v in nodes]
        kept = [times(self_w[0, level, n], parts[n]) for n in range(count)]
        sent = [times(cross_w[0, level, n], parts[n]) for n in range(count)]
        nodes = [masked(ranks[n], kept[n] + sent[n ^ (1 << level)]) for n in range(count)]
    for n in range(count):
        parts = split(nodes[n])
        keep_out[n] = times(self_w[0, 2, n], parts)
        sent = times(cross_w[0, 2, n], parts)
        if len(send_outs) == 1:
            send_outs[0][n] = sent
        else:
            send_outs[n][0] = sent


def local_levels(part, parts, arrays, coefficients, self_weights, cross_weights, ranks):
    _, count, rank, illum = coefficients.shape
    width = illum // parts
    block = 256
    steps = width // block
    mats = pl.BlockSpec((1, 3, count, rank, rank), lambda i, r: (0, 0, 0, 0, 0))
    out = pl.BlockSpec((count, rank, block), lambda i, r: (0, 0, i))
    return pl.pallas_call(
        local_kernel,
        grid_spec=pltpu.PrefetchScalarGridSpec(
            num_scalar_prefetch=1,
            grid=(steps,),
            in_specs=[
                pl.BlockSpec((1, count, rank, block), lambda i, r: (0, 0, 0, part * steps + i)),
                mats,
                mats,
            ],
            out_specs=[out]
            + [pl.BlockSpec((count // arrays, rank, block), lambda i, r: (0, 0, i))] * arrays,
        ),
        out_shape=[hbm(count, rank, width)] + [hbm(count // arrays, rank, width)] * arrays,
        compiler_params=params(),
        cost_estimate=COST,
        name=f"local_part{part}",
    )(ranks, *placed(coefficients, self_weights, cross_weights))


def widen_kernel(self_w, cross_w, *outs):
    each = 2 // len(outs)
    for n in range(2):
        outs[n // each][n % each, 0] = self_w[0, n, 0].astype(F32)
        outs[n // each][n % each, 1] = cross_w[0, n, 0].astype(F32)


def widen(node, arrays, self_weights, cross_weights):
    rank = self_weights.shape[-1]
    shape = (2 // arrays, 2, rank, rank)
    mats = pl.BlockSpec((1, 2, 1, rank, rank), lambda i: (0, 2, node, 0, 0))
    return pl.pallas_call(
        widen_kernel,
        grid=(1,),
        in_specs=[mats, mats],
        out_specs=[pl.BlockSpec(shape, lambda i: (0, 0, 0, 0))] * arrays,
        out_shape=[hbm(*shape)] * arrays,
        compiler_params=params(),
        cost_estimate=COST,
        name=f"widen_{node}",
    )(*placed(self_weights, cross_weights))


def level3_kernel(node, count, info, *refs):
    self_w, cross_w, keep_out, send_out = refs[2 * count :]
    taken = info[4] != 0
    keep_w = jnp.where(taken, cross_w[0, 0, 0], self_w[0, 0, 0])
    send_w = jnp.where(taken, self_w[0, 0, 0], cross_w[0, 0, 0])
    step = pl.program_id(0)
    steps = pl.num_programs(0) // count
    for c in range(count):

        @pl.when(step // steps == c)
        def _():
            parts = split(masked(info[node], refs[2 * c][0] + refs[2 * c + 1][0]))
            keep_out[...] = times(keep_w, parts)
            send_out[...] = times(send_w, parts)


def level3(node, info, pairs, self_weights, cross_weights):
    _, rank, width = pairs[0][0].shape
    count = len(pairs)
    block = 256
    steps = width // block

    def tiles(c):
        def at(i):
            return jnp.clip(i - c * steps, 0, steps - 1)

        return [
            pl.BlockSpec((1, rank, block), lambda i, r, n=n: (n, 0, at(i)))
            for n in (node, node if pairs[c][1].shape[0] > 1 else 0)
        ]

    mat = pl.BlockSpec((1, 1, 1, rank, rank), lambda i, r: (0, 3, node, 0, 0))
    out = pl.BlockSpec((rank, block), lambda i, r: (0, i))
    return pl.pallas_call(
        lambda *refs: level3_kernel(node, count, *refs),
        grid_spec=pltpu.PrefetchScalarGridSpec(
            num_scalar_prefetch=1,
            grid=(count * steps,),
            in_specs=[tile for c in range(count) for tile in tiles(c)] + [mat, mat],
            out_specs=[out, out],
        ),
        out_shape=[hbm(rank, count * width)] * 2,
        compiler_params=params(),
        cost_estimate=COST,
        name=f"level3_{node}",
    )(info, *[v for pair in pairs for v in pair], *placed(self_weights, cross_weights))


def moved_kernel(node, count, info, *refs):
    self_w, cross_w, moved, keep_out, send_out, mats = refs[2 * count :]
    step = pl.program_id(0)

    @pl.when(step == 0)
    def _():
        @pl.when(info[4] == 0)
        def _():
            mats[0] = self_w[0, 0, 0]
            mats[1] = cross_w[0, 0, 0]

        @pl.when(info[4] != 0)
        def _():
            mats[0] = moved[0, 0].astype(BF16)
            mats[1] = moved[0, 1].astype(BF16)

    steps = pl.num_programs(0) // count
    for c in range(count):

        @pl.when(step // steps == c)
        def _():
            parts = split(masked(info[node], refs[2 * c][...] + refs[2 * c + 1][...]))
            keep_out[...] = times(mats[0], parts)
            send_out[...] = times(mats[1], parts)


def moved_level(level, node, info, pairs, self_weights, cross_weights, moved):
    rank, width = pairs[0][0].shape
    count = len(pairs)
    block = 256
    steps = width // block
    spot = level - 4 if moved.shape[0] == 2 else 0

    def tile(c):
        return pl.BlockSpec(
            (rank, block), lambda i, r: (0, jnp.clip(i - c * steps, 0, steps - 1))
        )

    mat = pl.BlockSpec((1, 1, 1, rank, rank), lambda i, r: (0, level, node, 0, 0))
    out = pl.BlockSpec((rank, block), lambda i, r: (0, i))
    return pl.pallas_call(
        lambda *refs: moved_kernel(node, count, *refs),
        grid_spec=pltpu.PrefetchScalarGridSpec(
            num_scalar_prefetch=1,
            grid=(count * steps,),
            in_specs=[tile(c) for c in range(count) for _ in range(2)]
            + [mat, mat, pl.BlockSpec((1, 2, rank, rank), lambda i, r: (spot, 0, 0, 0))],
            out_specs=[out, out],
            scratch_shapes=[pltpu.VMEM((2, rank, rank), BF16)],
        ),
        out_shape=[hbm(rank, count * width)] * 2,
        compiler_params=params(),
        cost_estimate=COST,
        name=f"level{level}_{node}",
    )(info, *[v for pair in pairs for v in pair], *placed(self_weights, cross_weights), moved)


def total_kernel(node, count, info, *refs):
    out = refs[-1]
    step = pl.program_id(0)
    steps = pl.num_programs(0) // count
    block = out.shape[2]
    for c in range(count):

        @pl.when(step // steps == c)
        def _():
            value = masked(info[node], refs[2 * c][...] + refs[2 * c + 1][...])
            for j in range(out.shape[0]):
                out[j] = value[:, j * block : (j + 1) * block]


def total(node, info, pairs, cols):
    rank, width = pairs[0][0].shape
    count = len(pairs)
    block = count * width // cols
    each = 4
    steps = cols // (count * each)

    def tile(c):
        return pl.BlockSpec(
            (rank, each * block), lambda i, r: (0, jnp.clip(i - c * steps, 0, steps - 1))
        )

    return pl.pallas_call(
        lambda *refs: total_kernel(node, count, *refs),
        grid_spec=pltpu.PrefetchScalarGridSpec(
            num_scalar_prefetch=1,
            grid=(count * steps,),
            in_specs=[tile(c) for c in range(count) for _ in range(2)],
            out_specs=pl.BlockSpec((each, rank, block), lambda i, r: (i, 0, 0)),
        ),
        out_shape=hbm(cols, rank, block),
        compiler_params=params(),
        cost_estimate=COST,
        name=f"total_{node}",
    )(info, *[v for pair in pairs for v in pair])


def halve_kernel(node, spot, info, kept_a, recv_a, kept_b, recv_b, keep_out, send_out):
    for kept, recv, out in ((kept_a, recv_a, keep_out), (kept_b, recv_b, send_out)):
        total = kept[...] + recv[...]
        out[...] = total if node is None else masked(info[node], total)


def halve(node, spot, info, kept, recv, groups=1):
    rank, width = kept.shape
    block = width // (2 * groups)
    mine = pl.BlockSpec((rank, block), lambda i, s, r: (0, 2 * i + s[0]))
    theirs = pl.BlockSpec((rank, block), lambda i, s, r: (0, 2 * i + s[1]))
    out = pl.BlockSpec((rank, block), lambda i, s, r: (0, i))
    return pl.pallas_call(
        lambda *refs: halve_kernel(node, *refs),
        grid_spec=pltpu.PrefetchScalarGridSpec(
            num_scalar_prefetch=2,
            grid=(groups,),
            in_specs=[mine, mine, theirs, theirs],
            out_specs=[out, out],
        ),
        out_shape=[hbm(rank, groups * block)] * 2,
        compiler_params=params(),
        cost_estimate=COST,
        name="halve",
    )(spot, info, kept, recv, kept, recv)


def swap(value, axis, mask, chosen=lambda index: True):
    pairs = [(i, i ^ mask) for i in range(lax.axis_size(axis)) if chosen(i)]
    return lax.ppermute(value, axis, pairs)


def tie(value, *before):
    return lax.optimization_barrier((value, *before))[0]


CORE, Z1, Z2, X0 = 1, 2, 4, 8
PARTS = 2


def moves(index):
    return (index & 1) == ((index >> 2) & 1)


def shards(coefficients, self_weights, cross_weights, true_ranks):
    ranks = true_ranks[0]
    count = ranks.shape[0]
    nodes, cols = lax.axis_size("node"), lax.axis_size("col")
    col = lax.axis_index("col")
    y0, y1, z0 = col & 1, (col >> 1) & 1, (col >> 2) & 1
    home, across = [], []
    for d in range(nodes):
        to = d ^ Z1 if moves(d) else d
        for c in range(cols):
            across.append((d * cols + c, to * cols + (c ^ 4)))
            if moves(d):
                home.append((d * cols + c, to * cols + c))
    flag = moves(lax.axis_index("node")).astype(jnp.int32)
    weights = (self_weights, cross_weights)

    wide = [widen(0, 1, *weights)[0]]
    moved = {0: swap(wide[0], "node", Z1, moves)}
    pieces = [(0, (0,)), (0, (1,)), (1, (0,)), (1, (1,)), (2, (0,)), (2, (1,)), (3, (0,)), (3, (1,))]
    final = len(pieces)
    sends, fetches, arrivals = {1: 1, 2: 2, 3: 3, 4: 4, 5: 5, 6: 6, 7: 7}, {0: 1, 2: 2, 4: 3}, {3: 1, 5: 2, 7: 3}
    fifths, summing = {4: (0, [0, 1]), 6: (1, [2, 3]), 7: (2, [4, 5])}, {5: 0, 7: 1}

    own_info = jnp.concatenate([ranks, flag[None]])
    kept3, sent3, first = {}, {}, []

    def third(turn):
        node, held_parts = pieces[turn]
        kept3[turn], sent3[turn] = level3(node, own_info, [first[p] for p in held_parts], *weights)

    for part in range(PARTS):
        start = tie(ranks, sent3[0] if part else wide[0])
        k, sent = local_levels(part, PARTS, 1, coefficients, *weights, start)
        first.append((k, swap(sent, "node", CORE)))
        if part == pieces[0][1][-1]:
            third(0)
    later_ranks, later_weights = tie(ranks, sent3[0]), tie(self_weights, sent3[0])
    wide += [widen(node, 1, later_weights, cross_weights)[0] for node in range(1, count)]
    other_ranks = swap(later_ranks, "node", Z1, moves)
    held = jnp.where(flag == 1, other_ranks, ranks)
    held_info = jnp.concatenate([held, flag[None]])
    for turn in range(1, final):
        third(turn)
    r3 = {turn: swap(sent3[turn], "node", Z1) for turn in (0,)}
    if 0 in fetches:
        moved[fetches[0]] = swap(tie(wide[fetches[0]], sent3[0]), "node", Z1, moves)
    kept4, sent4, r4, fives, sums, blocks_of = {}, {}, {}, {}, [], []

    def fourth(turn):
        node = pieces[turn][0]
        k, s = moved_level(4, node, held_info, [(kept3[turn], r3[turn])], *weights, moved[node])
        if 0 and 0 <= turn < final - 1:
            s = tie(s, r4[turn - 0])
        kept4[turn], sent4[turn], r4[turn] = k, s, swap(s, "node", Z1 | Z2)

    def fifth(node, turns, *before):
        state = [(kept4[t], r4[t]) for t in turns]
        if before:
            state[0] = (tie(state[0][0], *before), state[0][1])
        k, s = moved_level(5, node, held_info, state, *weights, moved[node])
        return k, swap(s, "node", X0)

    def column_sum(node, terms):
        blocks = total(node, held_info, terms, cols)
        blocks_of.append(blocks)
        sums.append(jnp.sum(lax.all_to_all(blocks, "col", 0, 0, tiled=True), axis=0))

    def homeward(mine):
        return jnp.where(flag == 1, swap(mine, "node", Z1, moves), mine)

    for turn in range(1, final):
        values = {"r3": r3[turn - 1]}
        if turn in sends:
            values["sent3"] = sent3[sends[turn]]
        if turn in fetches:
            values["wide"] = wide[fetches[turn]]
        if turn in arrivals:
            values["moved"] = moved[arrivals[turn]]
        if 3 and turn >= 3:
            values["r4"] = r4[turn - 3]
        if turn == 7:
            values["sum"] = sums[0]
        summed = summing.get(turn)
        if summed is not None:
            values["five"] = fives[summed][1]
        values = dict(zip(values, lax.optimization_barrier(tuple(values.values()))))
        r3[turn - 1] = values["r3"]
        if turn in sends:
            r3[sends[turn]] = swap(values["sent3"], "node", Z1)
        if turn in arrivals:
            moved[arrivals[turn]] = values["moved"]
        if turn in fetches:
            moved[fetches[turn]] = swap(values["wide"], "node", Z1, moves)
        if "r4" in values:
            r4[turn - 3] = values["r4"]
        if "sum" in values:
            sums[0] = values["sum"]
        fourth(turn - 1)
        if turn in fifths:
            node, turns = fifths[turn]
            fives[node] = fifth(node, turns, *([sent4[turn - 1]] if False else []))
        if summed is not None:
            column_sum(summed, [(fives[summed][0], values["five"])])

    r3[final - 1], sums[1] = lax.optimization_barrier((r3[final - 1], sums[1]))
    fourth(final - 1)
    ends = [fifth(count - 1, [final - 2], *([sent4[final - 1]] if False else []))]
    column_sum(count - 2, [fives[count - 2]])
    kept4[final - 1] = tie(kept4[final - 1], blocks_of[-1])
    ends.append(fifth(count - 1, [final - 1]))
    early = jnp.stack(sums)

    def spot(bit):
        return jnp.stack([bit, 1 - bit]).astype(jnp.int32)

    quarters, before = [], [early] if False else []
    for k, r in ends:
        if quarters and before:
            k = tie(k, *before)
        k, s = halve(count - 1, spot(y1), held_info, k, r)
        k, s = halve(None, spot(y0), held_info, k, swap(s, "col", 2))
        if False:
            before.append(s)
        quarters.append(k + swap(s, "col", 1))
    mine = jnp.where(z0 == 1, quarters[1], quarters[0])
    theirs = jnp.where(z0 == 1, quarters[0], quarters[1])
    away = lax.ppermute(mine, ("node", "col"), home)
    other = lax.ppermute(theirs, ("node", "col"), across)
    end = jnp.where(flag == 1, away, mine) + other
    return jnp.concatenate([homeward(early), end[None]])


def solution(mesh):
    placed = (
        P("col", "node", None, None),
        P("col", None, "node", None, None),
        P("col", None, "node", None, None),
        P("col", "node"),
    )
    return jax.shard_map(
        shards, mesh=mesh, in_specs=placed, out_specs=P("node", None, "col"), check_vma=False
    )
```

```python
import jax
import jax.numpy as jnp
from jax import lax
from jax.experimental import pallas as pl
from jax.experimental.pallas import tpu as pltpu
from jax.sharding import PartitionSpec as P

F32 = jnp.float32
BF16 = jnp.bfloat16
VMEM_LIMIT = 48 * 1024 * 1024


def params():
    return pltpu.CompilerParams(vmem_limit_bytes=VMEM_LIMIT)


COST = pl.CostEstimate(flops=10**11, bytes_accessed=10**9, transcendentals=0)


def split(state):
    hi = state.astype(BF16)
    return jnp.concatenate([hi, (state - hi.astype(F32)).astype(BF16)], axis=0)


def times(weight, pieces):
    doubled = jnp.concatenate([weight, weight], axis=1)
    return jnp.dot(doubled, pieces, preferred_element_type=F32)


def masked(rank, value):
    return jnp.where(lax.broadcasted_iota(jnp.int32, value.shape, 0) < rank, value, 0.0)


def hbm(*shape):
    return pltpu.HBM(shape, F32)


def placed(*arrays):
    return [pltpu.with_memory_space_constraint(array, pltpu.HBM) for array in arrays]


def local_kernel(ranks, state, self_w, cross_w, keep_out, *send_outs):
    count = state.shape[1]
    nodes = [state[0, n] for n in range(count)]
    for level in range(2):
        parts = [split(v) for v in nodes]
        kept = [times(self_w[0, level, n], parts[n]) for n in range(count)]
        sent = [times(cross_w[0, level, n], parts[n]) for n in range(count)]
        nodes = [masked(ranks[n], kept[n] + sent[n ^ (1 << level)]) for n in range(count)]
    for n in range(count):
        parts = split(nodes[n])
        keep_out[n] = times(self_w[0, 2, n], parts)
        sent = times(cross_w[0, 2, n], parts)
        if len(send_outs) == 1:
            send_outs[0][n] = sent
        else:
            send_outs[n][0] = sent


def local_levels(part, parts, arrays, coefficients, self_weights, cross_weights, ranks):
    _, count, rank, illum = coefficients.shape
    width = illum // parts
    block = 256
    steps = width // block
    mats = pl.BlockSpec((1, 3, count, rank, rank), lambda i, r: (0, 0, 0, 0, 0))
    out = pl.BlockSpec((count, rank, block), lambda i, r: (0, 0, i))
    return pl.pallas_call(
        local_kernel,
        grid_spec=pltpu.PrefetchScalarGridSpec(
            num_scalar_prefetch=1,
            grid=(steps,),
            in_specs=[
                pl.BlockSpec((1, count, rank, block), lambda i, r: (0, 0, 0, part * steps + i)),
                mats,
                mats,
            ],
            out_specs=[out]
            + [pl.BlockSpec((count // arrays, rank, block), lambda i, r: (0, 0, i))] * arrays,
        ),
        out_shape=[hbm(count, rank, width)] + [hbm(count // arrays, rank, width)] * arrays,
        compiler_params=params(),
        cost_estimate=COST,
        name=f"local_part{part}",
    )(ranks, *placed(coefficients, self_weights, cross_weights))


def widen_kernel(self_w, cross_w, *outs):
    each = 2 // len(outs)
    for n in range(2):
        outs[n // each][n % each, 0] = self_w[0, n, 0].astype(F32)
        outs[n // each][n % each, 1] = cross_w[0, n, 0].astype(F32)


def widen(node, arrays, self_weights, cross_weights):
    rank = self_weights.shape[-1]
    shape = (2 // arrays, 2, rank, rank)
    mats = pl.BlockSpec((1, 2, 1, rank, rank), lambda i: (0, 2, node, 0, 0))
    return pl.pallas_call(
        widen_kernel,
        grid=(1,),
        in_specs=[mats, mats],
        out_specs=[pl.BlockSpec(shape, lambda i: (0, 0, 0, 0))] * arrays,
        out_shape=[hbm(*shape)] * arrays,
        compiler_params=params(),
        cost_estimate=COST,
        name=f"widen_{node}",
    )(*placed(self_weights, cross_weights))


def level3_kernel(node, count, info, *refs):
    self_w, cross_w, keep_out, send_out = refs[2 * count :]
    taken = info[4] != 0
    keep_w = jnp.where(taken, cross_w[0, 0, 0], self_w[0, 0, 0])
    send_w = jnp.where(taken, self_w[0, 0, 0], cross_w[0, 0, 0])
    step = pl.program_id(0)
    steps = pl.num_programs(0) // count
    for c in range(count):

        @pl.when(step // steps == c)
        def _():
            parts = split(masked(info[node], refs[2 * c][0] + refs[2 * c + 1][0]))
            keep_out[...] = times(keep_w, parts)
            send_out[...] = times(send_w, parts)


def level3(node, info, pairs, self_weights, cross_weights):
    _, rank, width = pairs[0][0].shape
    count = len(pairs)
    block = 256
    steps = width // block

    def tiles(c):
        def at(i):
            return jnp.clip(i - c * steps, 0, steps - 1)

        return [
            pl.BlockSpec((1, rank, block), lambda i, r, n=n: (n, 0, at(i)))
            for n in (node, node if pairs[c][1].shape[0] > 1 else 0)
        ]

    mat = pl.BlockSpec((1, 1, 1, rank, rank), lambda i, r: (0, 3, node, 0, 0))
    out = pl.BlockSpec((rank, block), lambda i, r: (0, i))
    return pl.pallas_call(
        lambda *refs: level3_kernel(node, count, *refs),
        grid_spec=pltpu.PrefetchScalarGridSpec(
            num_scalar_prefetch=1,
            grid=(count * steps,),
            in_specs=[tile for c in range(count) for tile in tiles(c)] + [mat, mat],
            out_specs=[out, out],
        ),
        out_shape=[hbm(rank, count * width)] * 2,
        compiler_params=params(),
        cost_estimate=COST,
        name=f"level3_{node}",
    )(info, *[v for pair in pairs for v in pair], *placed(self_weights, cross_weights))


def moved_kernel(node, count, info, *refs):
    self_w, cross_w, moved, keep_out, send_out, mats = refs[2 * count :]
    step = pl.program_id(0)

    @pl.when(step == 0)
    def _():
        @pl.when(info[4] == 0)
        def _():
            mats[0] = self_w[0, 0, 0]
            mats[1] = cross_w[0, 0, 0]

        @pl.when(info[4] != 0)
        def _():
            mats[0] = moved[0, 0].astype(BF16)
            mats[1] = moved[0, 1].astype(BF16)

    steps = pl.num_programs(0) // count
    for c in range(count):

        @pl.when(step // steps == c)
        def _():
            parts = split(masked(info[node], refs[2 * c][...] + refs[2 * c + 1][...]))
            keep_out[...] = times(mats[0], parts)
            send_out[...] = times(mats[1], parts)


def moved_level(level, node, info, pairs, self_weights, cross_weights, moved):
    rank, width = pairs[0][0].shape
    count = len(pairs)
    block = 256
    steps = width // block
    spot = level - 4 if moved.shape[0] == 2 else 0

    def tile(c):
        return pl.BlockSpec(
            (rank, block), lambda i, r: (0, jnp.clip(i - c * steps, 0, steps - 1))
        )

    mat = pl.BlockSpec((1, 1, 1, rank, rank), lambda i, r: (0, level, node, 0, 0))
    out = pl.BlockSpec((rank, block), lambda i, r: (0, i))
    return pl.pallas_call(
        lambda *refs: moved_kernel(node, count, *refs),
        grid_spec=pltpu.PrefetchScalarGridSpec(
            num_scalar_prefetch=1,
            grid=(count * steps,),
            in_specs=[tile(c) for c in range(count) for _ in range(2)]
            + [mat, mat, pl.BlockSpec((1, 2, rank, rank), lambda i, r: (spot, 0, 0, 0))],
            out_specs=[out, out],
            scratch_shapes=[pltpu.VMEM((2, rank, rank), BF16)],
        ),
        out_shape=[hbm(rank, count * width)] * 2,
        compiler_params=params(),
        cost_estimate=COST,
        name=f"level{level}_{node}",
    )(info, *[v for pair in pairs for v in pair], *placed(self_weights, cross_weights), moved)


def total_kernel(node, count, info, *refs):
    out = refs[-1]
    step = pl.program_id(0)
    steps = pl.num_programs(0) // count
    block = out.shape[2]
    for c in range(count):

        @pl.when(step // steps == c)
        def _():
            value = masked(info[node], refs[2 * c][...] + refs[2 * c + 1][...])
            for j in range(out.shape[0]):
                out[j] = value[:, j * block : (j + 1) * block]


def total(node, info, pairs, cols):
    rank, width = pairs[0][0].shape
    count = len(pairs)
    block = count * width // cols
    each = 4
    steps = cols // (count * each)

    def tile(c):
        return pl.BlockSpec(
            (rank, each * block), lambda i, r: (0, jnp.clip(i - c * steps, 0, steps - 1))
        )

    return pl.pallas_call(
        lambda *refs: total_kernel(node, count, *refs),
        grid_spec=pltpu.PrefetchScalarGridSpec(
            num_scalar_prefetch=1,
            grid=(count * steps,),
            in_specs=[tile(c) for c in range(count) for _ in range(2)],
            out_specs=pl.BlockSpec((each, rank, block), lambda i, r: (i, 0, 0)),
        ),
        out_shape=hbm(cols, rank, block),
        compiler_params=params(),
        cost_estimate=COST,
        name=f"total_{node}",
    )(info, *[v for pair in pairs for v in pair])


def halve_kernel(node, spot, info, kept_a, recv_a, kept_b, recv_b, keep_out, send_out):
    for kept, recv, out in ((kept_a, recv_a, keep_out), (kept_b, recv_b, send_out)):
        total = kept[...] + recv[...]
        out[...] = total if node is None else masked(info[node], total)


def halve(node, spot, info, kept, recv, groups=1):
    rank, width = kept.shape
    block = width // (2 * groups)
    mine = pl.BlockSpec((rank, block), lambda i, s, r: (0, 2 * i + s[0]))
    theirs = pl.BlockSpec((rank, block), lambda i, s, r: (0, 2 * i + s[1]))
    out = pl.BlockSpec((rank, block), lambda i, s, r: (0, i))
    return pl.pallas_call(
        lambda *refs: halve_kernel(node, *refs),
        grid_spec=pltpu.PrefetchScalarGridSpec(
            num_scalar_prefetch=2,
            grid=(groups,),
            in_specs=[mine, mine, theirs, theirs],
            out_specs=[out, out],
        ),
        out_shape=[hbm(rank, groups * block)] * 2,
        compiler_params=params(),
        cost_estimate=COST,
        name="halve",
    )(spot, info, kept, recv, kept, recv)


def swap(value, axis, mask, chosen=lambda index: True):
    pairs = [(i, i ^ mask) for i in range(lax.axis_size(axis)) if chosen(i)]
    return lax.ppermute(value, axis, pairs)


def tie(value, *before):
    return lax.optimization_barrier((value, *before))[0]


CORE, Z1, Z2, X0 = 1, 2, 4, 8
PARTS = 2


def moves(index):
    return (index & 1) == ((index >> 2) & 1)


def shards(coefficients, self_weights, cross_weights, true_ranks):
    ranks = true_ranks[0]
    count = ranks.shape[0]
    nodes, cols = lax.axis_size("node"), lax.axis_size("col")
    col = lax.axis_index("col")
    y0, y1, z0 = col & 1, (col >> 1) & 1, (col >> 2) & 1
    home, across = [], []
    for d in range(nodes):
        to = d ^ Z1 if moves(d) else d
        for c in range(cols):
            across.append((d * cols + c, to * cols + (c ^ 4)))
            if moves(d):
                home.append((d * cols + c, to * cols + c))
    flag = moves(lax.axis_index("node")).astype(jnp.int32)
    weights = (self_weights, cross_weights)

    wide = {}
    wide[4, 0] = wide[5, 0] = widen(0, 1, *weights)[0]
    moved = {}
    moved[4, 0] = moved[5, 0] = swap(wide[4, 0], "node", Z1, moves)
    pieces = [(0, (0,)), (0, (1,)), (1, (0,)), (1, (1,)), (2, (0,)), (2, (1,)), (3, (0,)), (3, (1,))]
    final = len(pieces)
    sends, fetches, arrivals = {1: 1, 2: 2, 3: 3, 4: 4, 5: 5, 6: 6, 7: 7}, {1: (4, 1), 2: (5, 1), 3: (4, 2), 4: (5, 2), 5: (4, 3), 6: (5, 3)}, {3: (4, 1), 4: (5, 1), 5: (4, 2), 6: (5, 2), 7: (4, 3)}
    fifths, summing = {4: (0, [0, 1]), 6: (1, [2, 3]), 7: (2, [4, 5])}, {5: 0, 7: 1}

    own_info = jnp.concatenate([ranks, flag[None]])
    kept3, sent3, first = {}, {}, []

    def third(turn):
        node, held_parts = pieces[turn]
        kept3[turn], sent3[turn] = level3(node, own_info, [first[p] for p in held_parts], *weights)

    for part in range(PARTS):
        start = tie(ranks, sent3[0] if part else wide[4, 0])
        k, sent = local_levels(part, PARTS, 1, coefficients, *weights, start)
        first.append((k, swap(sent, "node", CORE)))
        if part == pieces[0][1][-1]:
            third(0)
    later_ranks, later_weights = tie(ranks, sent3[0]), tie(self_weights, sent3[0])
    for node in range(1, count):
        wide[4, node], wide[5, node] = widen(node, 2, later_weights, cross_weights)
    other_ranks = swap(later_ranks, "node", Z1, moves)
    held = jnp.where(flag == 1, other_ranks, ranks)
    held_info = jnp.concatenate([held, flag[None]])
    for turn in range(1, final):
        third(turn)
    r3 = {turn: swap(sent3[turn], "node", Z1) for turn in (0,)}
    if 0 in fetches:
        moved[fetches[0]] = swap(tie(wide[fetches[0]], sent3[0]), "node", Z1, moves)
    kept4, sent4, r4, fives, sums, blocks_of = {}, {}, {}, {}, [], []

    def fourth(turn):
        node = pieces[turn][0]
        k, s = moved_level(4, node, held_info, [(kept3[turn], r3[turn])], *weights, moved[4, node])
        if 0 and 0 <= turn < final - 1:
            s = tie(s, r4[turn - 0])
        kept4[turn], sent4[turn], r4[turn] = k, s, swap(s, "node", Z1 | Z2)

    def fifth(node, turns, *before):
        state = [(kept4[t], r4[t]) for t in turns]
        if before:
            state[0] = (tie(state[0][0], *before), state[0][1])
        k, s = moved_level(5, node, held_info, state, *weights, moved[5, node])
        return k, swap(s, "node", X0)

    def column_sum(node, terms):
        blocks = total(node, held_info, terms, cols)
        blocks_of.append(blocks)
        sums.append(jnp.sum(lax.all_to_all(blocks, "col", 0, 0, tiled=True), axis=0))

    def homeward(mine):
        return jnp.where(flag == 1, swap(mine, "node", Z1, moves), mine)

    for turn in range(1, final):
        values = {"r3": r3[turn - 1]}
        if turn in sends:
            values["sent3"] = sent3[sends[turn]]
        if turn in fetches:
            values["wide"] = wide[fetches[turn]]
        if turn in arrivals:
            values["moved"] = moved[arrivals[turn]]
        if 3 and turn >= 3:
            values["r4"] = r4[turn - 3]
        if turn == 7:
            values["sum"] = sums[0]
        summed = summing.get(turn)
        if summed is not None:
            values["five"] = fives[summed][1]
        values = dict(zip(values, lax.optimization_barrier(tuple(values.values()))))
        r3[turn - 1] = values["r3"]
        if turn in sends:
            r3[sends[turn]] = swap(values["sent3"], "node", Z1)
        if turn in arrivals:
            moved[arrivals[turn]] = values["moved"]
        if turn in fetches:
            moved[fetches[turn]] = swap(values["wide"], "node", Z1, moves)
        if "r4" in values:
            r4[turn - 3] = values["r4"]
        if "sum" in values:
            sums[0] = values["sum"]
        fourth(turn - 1)
        if turn in fifths:
            node, turns = fifths[turn]
            fives[node] = fifth(node, turns, *([sent4[turn - 1]] if False else []))
        if summed is not None:
            column_sum(summed, [(fives[summed][0], values["five"])])

    r3[final - 1], sums[1] = lax.optimization_barrier((r3[final - 1], sums[1]))
    fourth(final - 1)
    ends = [fifth(count - 1, [final - 2], *([sent4[final - 1]] if False else []))]
    column_sum(count - 2, [fives[count - 2]])
    kept4[final - 1] = tie(kept4[final - 1], blocks_of[-1])
    ends.append(fifth(count - 1, [final - 1]))
    early = jnp.stack(sums)

    def spot(bit):
        return jnp.stack([bit, 1 - bit]).astype(jnp.int32)

    quarters, before = [], [early] if True else []
    for k, r in ends:
        if quarters and before:
            k = tie(k, *before)
        k, s = halve(count - 1, spot(y1), held_info, k, r)
        k, s = halve(None, spot(y0), held_info, k, swap(s, "col", 2))
        if False:
            before.append(s)
        quarters.append(k + swap(s, "col", 1))
    mine = jnp.where(z0 == 1, quarters[1], quarters[0])
    theirs = jnp.where(z0 == 1, quarters[0], quarters[1])
    away = lax.ppermute(mine, ("node", "col"), home)
    other = lax.ppermute(theirs, ("node", "col"), across)
    end = jnp.where(flag == 1, away, mine) + other
    return jnp.concatenate([homeward(early), end[None]])


def solution(mesh):
    placed = (
        P("col", "node", None, None),
        P("col", None, "node", None, None),
        P("col", None, "node", None, None),
        P("col", "node"),
    )
    return jax.shard_map(
        shards, mesh=mesh, in_specs=placed, out_specs=P("node", None, "col"), check_vma=False
    )
```

```python
import jax
import jax.numpy as jnp
from jax import lax
from jax.experimental import pallas as pl
from jax.experimental.pallas import tpu as pltpu
from jax.sharding import PartitionSpec as P

F32 = jnp.float32
BF16 = jnp.bfloat16
VMEM_LIMIT = 48 * 1024 * 1024


def params():
    return pltpu.CompilerParams(vmem_limit_bytes=VMEM_LIMIT)


COST = pl.CostEstimate(flops=10**11, bytes_accessed=10**9, transcendentals=0)


def split(state):
    hi = state.astype(BF16)
    return jnp.concatenate([hi, (state - hi.astype(F32)).astype(BF16)], axis=0)


def times(weight, pieces):
    doubled = jnp.concatenate([weight, weight], axis=1)
    return jnp.dot(doubled, pieces, preferred_element_type=F32)


def masked(rank, value):
    return jnp.where(lax.broadcasted_iota(jnp.int32, value.shape, 0) < rank, value, 0.0)


def hbm(*shape):
    return pltpu.HBM(shape, F32)


def placed(*arrays):
    return [pltpu.with_memory_space_constraint(array, pltpu.HBM) for array in arrays]


def local_kernel(ranks, state, self_w, cross_w, keep_out, *send_outs):
    count = state.shape[1]
    nodes = [state[0, n] for n in range(count)]
    for level in range(2):
        parts = [split(v) for v in nodes]
        kept = [times(self_w[0, level, n], parts[n]) for n in range(count)]
        sent = [times(cross_w[0, level, n], parts[n]) for n in range(count)]
        nodes = [masked(ranks[n], kept[n] + sent[n ^ (1 << level)]) for n in range(count)]
    for n in range(count):
        parts = split(nodes[n])
        keep_out[n] = times(self_w[0, 2, n], parts)
        sent = times(cross_w[0, 2, n], parts)
        if len(send_outs) == 1:
            send_outs[0][n] = sent
        else:
            send_outs[n][0] = sent


def local_levels(part, parts, arrays, coefficients, self_weights, cross_weights, ranks):
    _, count, rank, illum = coefficients.shape
    width = illum // parts
    block = 256
    steps = width // block
    mats = pl.BlockSpec((1, 3, count, rank, rank), lambda i, r: (0, 0, 0, 0, 0))
    out = pl.BlockSpec((count, rank, block), lambda i, r: (0, 0, i))
    return pl.pallas_call(
        local_kernel,
        grid_spec=pltpu.PrefetchScalarGridSpec(
            num_scalar_prefetch=1,
            grid=(steps,),
            in_specs=[
                pl.BlockSpec((1, count, rank, block), lambda i, r: (0, 0, 0, part * steps + i)),
                mats,
                mats,
            ],
            out_specs=[out]
            + [pl.BlockSpec((count // arrays, rank, block), lambda i, r: (0, 0, i))] * arrays,
        ),
        out_shape=[hbm(count, rank, width)] + [hbm(count // arrays, rank, width)] * arrays,
        compiler_params=params(),
        cost_estimate=COST,
        name=f"local_part{part}",
    )(ranks, *placed(coefficients, self_weights, cross_weights))


def widen_kernel(self_w, cross_w, *outs):
    each = 2 // len(outs)
    for n in range(2):
        outs[n // each][n % each, 0] = self_w[0, n, 0].astype(F32)
        outs[n // each][n % each, 1] = cross_w[0, n, 0].astype(F32)


def widen(node, arrays, self_weights, cross_weights):
    rank = self_weights.shape[-1]
    shape = (2 // arrays, 2, rank, rank)
    mats = pl.BlockSpec((1, 2, 1, rank, rank), lambda i: (0, 2, node, 0, 0))
    return pl.pallas_call(
        widen_kernel,
        grid=(1,),
        in_specs=[mats, mats],
        out_specs=[pl.BlockSpec(shape, lambda i: (0, 0, 0, 0))] * arrays,
        out_shape=[hbm(*shape)] * arrays,
        compiler_params=params(),
        cost_estimate=COST,
        name=f"widen_{node}",
    )(*placed(self_weights, cross_weights))


def level3_kernel(node, count, info, *refs):
    self_w, cross_w, keep_out, send_out = refs[2 * count :]
    taken = info[4] != 0
    keep_w = jnp.where(taken, cross_w[0, 0, 0], self_w[0, 0, 0])
    send_w = jnp.where(taken, self_w[0, 0, 0], cross_w[0, 0, 0])
    step = pl.program_id(0)
    steps = pl.num_programs(0) // count
    for c in range(count):

        @pl.when(step // steps == c)
        def _():
            parts = split(masked(info[node], refs[2 * c][0] + refs[2 * c + 1][0]))
            keep_out[...] = times(keep_w, parts)
            send_out[...] = times(send_w, parts)


def level3(node, info, pairs, self_weights, cross_weights):
    _, rank, width = pairs[0][0].shape
    count = len(pairs)
    block = 256
    steps = width // block

    def tiles(c):
        def at(i):
            return jnp.clip(i - c * steps, 0, steps - 1)

        return [
            pl.BlockSpec((1, rank, block), lambda i, r, n=n: (n, 0, at(i)))
            for n in (node, node if pairs[c][1].shape[0] > 1 else 0)
        ]

    mat = pl.BlockSpec((1, 1, 1, rank, rank), lambda i, r: (0, 3, node, 0, 0))
    out = pl.BlockSpec((rank, block), lambda i, r: (0, i))
    return pl.pallas_call(
        lambda *refs: level3_kernel(node, count, *refs),
        grid_spec=pltpu.PrefetchScalarGridSpec(
            num_scalar_prefetch=1,
            grid=(count * steps,),
            in_specs=[tile for c in range(count) for tile in tiles(c)] + [mat, mat],
            out_specs=[out, out],
        ),
        out_shape=[hbm(rank, count * width)] * 2,
        compiler_params=params(),
        cost_estimate=COST,
        name=f"level3_{node}",
    )(info, *[v for pair in pairs for v in pair], *placed(self_weights, cross_weights))


def moved_kernel(node, count, info, *refs):
    self_w, cross_w, moved, keep_out, send_out, mats = refs[2 * count :]
    step = pl.program_id(0)

    @pl.when(step == 0)
    def _():
        @pl.when(info[4] == 0)
        def _():
            mats[0] = self_w[0, 0, 0]
            mats[1] = cross_w[0, 0, 0]

        @pl.when(info[4] != 0)
        def _():
            mats[0] = moved[0, 0].astype(BF16)
            mats[1] = moved[0, 1].astype(BF16)

    steps = pl.num_programs(0) // count
    for c in range(count):

        @pl.when(step // steps == c)
        def _():
            parts = split(masked(info[node], refs[2 * c][...] + refs[2 * c + 1][...]))
            keep_out[...] = times(mats[0], parts)
            send_out[...] = times(mats[1], parts)


def moved_level(level, node, info, pairs, self_weights, cross_weights, moved):
    rank, width = pairs[0][0].shape
    count = len(pairs)
    block = 256
    steps = width // block
    spot = level - 4 if moved.shape[0] == 2 else 0

    def tile(c):
        return pl.BlockSpec(
            (rank, block), lambda i, r: (0, jnp.clip(i - c * steps, 0, steps - 1))
        )

    mat = pl.BlockSpec((1, 1, 1, rank, rank), lambda i, r: (0, level, node, 0, 0))
    out = pl.BlockSpec((rank, block), lambda i, r: (0, i))
    return pl.pallas_call(
        lambda *refs: moved_kernel(node, count, *refs),
        grid_spec=pltpu.PrefetchScalarGridSpec(
            num_scalar_prefetch=1,
            grid=(count * steps,),
            in_specs=[tile(c) for c in range(count) for _ in range(2)]
            + [mat, mat, pl.BlockSpec((1, 2, rank, rank), lambda i, r: (spot, 0, 0, 0))],
            out_specs=[out, out],
            scratch_shapes=[pltpu.VMEM((2, rank, rank), BF16)],
        ),
        out_shape=[hbm(rank, count * width)] * 2,
        compiler_params=params(),
        cost_estimate=COST,
        name=f"level{level}_{node}",
    )(info, *[v for pair in pairs for v in pair], *placed(self_weights, cross_weights), moved)


def total_kernel(node, count, info, *refs):
    out = refs[-1]
    step = pl.program_id(0)
    steps = pl.num_programs(0) // count
    block = out.shape[2]
    for c in range(count):

        @pl.when(step // steps == c)
        def _():
            value = masked(info[node], refs[2 * c][...] + refs[2 * c + 1][...])
            for j in range(out.shape[0]):
                out[j] = value[:, j * block : (j + 1) * block]


def total(node, info, pairs, cols):
    rank, width = pairs[0][0].shape
    count = len(pairs)
    block = count * width // cols
    each = 4
    steps = cols // (count * each)

    def tile(c):
        return pl.BlockSpec(
            (rank, each * block), lambda i, r: (0, jnp.clip(i - c * steps, 0, steps - 1))
        )

    return pl.pallas_call(
        lambda *refs: total_kernel(node, count, *refs),
        grid_spec=pltpu.PrefetchScalarGridSpec(
            num_scalar_prefetch=1,
            grid=(count * steps,),
            in_specs=[tile(c) for c in range(count) for _ in range(2)],
            out_specs=pl.BlockSpec((each, rank, block), lambda i, r: (i, 0, 0)),
        ),
        out_shape=hbm(cols, rank, block),
        compiler_params=params(),
        cost_estimate=COST,
        name=f"total_{node}",
    )(info, *[v for pair in pairs for v in pair])


def halve_kernel(node, spot, info, kept_a, recv_a, kept_b, recv_b, keep_out, send_out):
    for kept, recv, out in ((kept_a, recv_a, keep_out), (kept_b, recv_b, send_out)):
        total = kept[...] + recv[...]
        out[...] = total if node is None else masked(info[node], total)


def halve(node, spot, info, kept, recv, groups=1):
    rank, width = kept.shape
    block = width // (2 * groups)
    mine = pl.BlockSpec((rank, block), lambda i, s, r: (0, 2 * i + s[0]))
    theirs = pl.BlockSpec((rank, block), lambda i, s, r: (0, 2 * i + s[1]))
    out = pl.BlockSpec((rank, block), lambda i, s, r: (0, i))
    return pl.pallas_call(
        lambda *refs: halve_kernel(node, *refs),
        grid_spec=pltpu.PrefetchScalarGridSpec(
            num_scalar_prefetch=2,
            grid=(groups,),
            in_specs=[mine, mine, theirs, theirs],
            out_specs=[out, out],
        ),
        out_shape=[hbm(rank, groups * block)] * 2,
        compiler_params=params(),
        cost_estimate=COST,
        name="halve",
    )(spot, info, kept, recv, kept, recv)


def swap(value, axis, mask, chosen=lambda index: True):
    pairs = [(i, i ^ mask) for i in range(lax.axis_size(axis)) if chosen(i)]
    return lax.ppermute(value, axis, pairs)


def tie(value, *before):
    return lax.optimization_barrier((value, *before))[0]


CORE, Z1, Z2, X0 = 1, 2, 4, 8
PARTS = 2


def moves(index):
    return (index & 1) == ((index >> 2) & 1)


def shards(coefficients, self_weights, cross_weights, true_ranks):
    ranks = true_ranks[0]
    count = ranks.shape[0]
    nodes, cols = lax.axis_size("node"), lax.axis_size("col")
    col = lax.axis_index("col")
    y0, y1, z0 = col & 1, (col >> 1) & 1, (col >> 2) & 1
    home, across = [], []
    for d in range(nodes):
        to = d ^ Z1 if moves(d) else d
        for c in range(cols):
            across.append((d * cols + c, to * cols + (c ^ 4)))
            if moves(d):
                home.append((d * cols + c, to * cols + c))
    flag = moves(lax.axis_index("node")).astype(jnp.int32)
    weights = (self_weights, cross_weights)

    wide = {}
    wide[4, 0] = wide[5, 0] = widen(0, 1, *weights)[0]
    moved = {}
    moved[4, 0] = moved[5, 0] = swap(wide[4, 0], "node", Z1, moves)
    pieces = [(0, (0,)), (0, (1,)), (1, (0,)), (1, (1,)), (2, (0,)), (2, (1,)), (3, (0,)), (3, (1,))]
    final = len(pieces)
    sends, fetches, arrivals = {1: 1, 2: 2, 3: 3, 4: 4, 5: 5, 6: 6, 7: 7}, {0: (4, 1), 2: (5, 1), 3: (4, 2), 4: (5, 2), 5: (4, 3), 6: (5, 3)}, {3: (4, 1), 4: (5, 1), 5: (4, 2), 6: (5, 2), 7: (4, 3)}
    fifths, summing = {4: (0, [0, 1]), 6: (1, [2, 3]), 7: (2, [4, 5])}, {5: 0, 7: 1}

    own_info = jnp.concatenate([ranks, flag[None]])
    kept3, sent3, first = {}, {}, []

    def third(turn):
        node, held_parts = pieces[turn]
        kept3[turn], sent3[turn] = level3(node, own_info, [first[p] for p in held_parts], *weights)

    for part in range(PARTS):
        start = tie(ranks, sent3[0] if part else wide[4, 0])
        k, sent = local_levels(part, PARTS, 1, coefficients, *weights, start)
        first.append((k, swap(sent, "node", CORE)))
        if part == pieces[0][1][-1]:
            third(0)
    later_ranks, later_weights = tie(ranks, sent3[0]), tie(self_weights, sent3[0])
    for node in range(1, count):
        wide[4, node], wide[5, node] = widen(node, 2, later_weights, cross_weights)
    other_ranks = swap(later_ranks, "node", Z1, moves)
    held = jnp.where(flag == 1, other_ranks, ranks)
    held_info = jnp.concatenate([held, flag[None]])
    for turn in range(1, final):
        third(turn)
    r3 = {turn: swap(sent3[turn], "node", Z1) for turn in (0,)}
    if 0 in fetches:
        moved[fetches[0]] = swap(tie(wide[fetches[0]], sent3[0]), "node", Z1, moves)
    kept4, sent4, r4, fives, sums, blocks_of = {}, {}, {}, {}, [], []

    def fourth(turn):
        node = pieces[turn][0]
        k, s = moved_level(4, node, held_info, [(kept3[turn], r3[turn])], *weights, moved[4, node])
        if 0 and 0 <= turn < final - 1:
            s = tie(s, r4[turn - 0])
        kept4[turn], sent4[turn], r4[turn] = k, s, swap(s, "node", Z1 | Z2)

    def fifth(node, turns, *before):
        state = [(kept4[t], r4[t]) for t in turns]
        if before:
            state[0] = (tie(state[0][0], *before), state[0][1])
        k, s = moved_level(5, node, held_info, state, *weights, moved[5, node])
        return k, swap(s, "node", X0)

    def column_sum(node, terms):
        blocks = total(node, held_info, terms, cols)
        blocks_of.append(blocks)
        sums.append(jnp.sum(lax.all_to_all(blocks, "col", 0, 0, tiled=True), axis=0))

    def homeward(mine):
        return jnp.where(flag == 1, swap(mine, "node", Z1, moves), mine)

    for turn in range(1, final):
        values = {"r3": r3[turn - 1]}
        if turn in sends:
            values["sent3"] = sent3[sends[turn]]
        if turn in fetches:
            values["wide"] = wide[fetches[turn]]
        if turn in arrivals:
            values["moved"] = moved[arrivals[turn]]
        if 3 and turn >= 3:
            values["r4"] = r4[turn - 3]
        if turn == 7:
            values["sum"] = sums[0]
        summed = summing.get(turn)
        if summed is not None:
            values["five"] = fives[summed][1]
        values = dict(zip(values, lax.optimization_barrier(tuple(values.values()))))
        r3[turn - 1] = values["r3"]
        if turn in sends:
            r3[sends[turn]] = swap(values["sent3"], "node", Z1)
        if turn in arrivals:
            moved[arrivals[turn]] = values["moved"]
        if turn in fetches:
            moved[fetches[turn]] = swap(values["wide"], "node", Z1, moves)
        if "r4" in values:
            r4[turn - 3] = values["r4"]
        if "sum" in values:
            sums[0] = values["sum"]
        fourth(turn - 1)
        if turn in fifths:
            node, turns = fifths[turn]
            fives[node] = fifth(node, turns, *([sent4[turn - 1]] if False else []))
        if summed is not None:
            column_sum(summed, [(fives[summed][0], values["five"])])

    r3[final - 1], sums[1] = lax.optimization_barrier((r3[final - 1], sums[1]))
    fourth(final - 1)
    ends = [fifth(count - 1, [final - 2], *([sent4[final - 1]] if False else []))]
    column_sum(count - 2, [fives[count - 2]])
    kept4[final - 1] = tie(kept4[final - 1], blocks_of[-1])
    ends.append(fifth(count - 1, [final - 1]))
    early = jnp.stack(sums)

    def spot(bit):
        return jnp.stack([bit, 1 - bit]).astype(jnp.int32)

    quarters, before = [], [early] if True else []
    for k, r in ends:
        if quarters and before:
            k = tie(k, *before)
        k, s = halve(count - 1, spot(y1), held_info, k, r)
        k, s = halve(None, spot(y0), held_info, k, swap(s, "col", 2))
        if False:
            before.append(s)
        quarters.append(k + swap(s, "col", 1))
    mine = jnp.where(z0 == 1, quarters[1], quarters[0])
    theirs = jnp.where(z0 == 1, quarters[0], quarters[1])
    away = lax.ppermute(mine, ("node", "col"), home)
    other = lax.ppermute(theirs, ("node", "col"), across)
    end = jnp.where(flag == 1, away, mine) + other
    return jnp.concatenate([homeward(early), end[None]])


def solution(mesh):
    placed = (
        P("col", "node", None, None),
        P("col", None, "node", None, None),
        P("col", None, "node", None, None),
        P("col", "node"),
    )
    return jax.shard_map(
        shards, mesh=mesh, in_specs=placed, out_specs=P("node", None, "col"), check_vma=False
    )
```
